512 devices in a mesh: row: 32 (over z, y_hi, core), col: 16 (over y_lo, x).
Axes of the slice: x: 4, y: 8 (y_hi: 2, y_lo: 4; y = y_hi * 4 + y_lo), z: 8, core: 2. Of those that a mesh axis runs over, the one named last changes fastest.
Arguments:
- blocks: bfloat16 [128, 192, 128, 128], P('row', 'col'), may hold values from -0.078125 to 0.078125
- columns: int32 [128, 192], P('row', 'col'), may hold values from 0 to 7
- counts: int32 [128, 16], P('row', 'col'), may hold values from 6 to 12, as said below
- inverse_diag: float32 [128, 128, 128], P('row')
- log_inverse_permeability: float32 [128, 128], P('row'), may hold values from -1 to 1
- base_velocity: float32 [128, 128], P('row'), may hold values from -6 to 6
- direction: float32 [32, 128, 128], P(None, 'row'), may hold values from -6 to 6
- obs_rows: int32 [4096], P('row'), may hold values from 0 to 3
- obs_weight: float32 [4096, 128], P('row'), may hold values from -0.5 to 0.5
- noise_prec: float32 [4096], P('row'), may hold values from 0.5 to 2
Outputs:
- hessian: float32 [32, 128, 128], P(None, 'row')
- predicted: float32 [32, 4096], P(None, 'row')
The draws below stay inside these ranges and needn't reach their ends.
Inputs may be any that keep to these rules, and one draw needn't show every extreme that they name: `counts`: every index of row has a block row with all 12 slots live in each column group.
All inputs are finite; a program needn't handle non-finite values.
Results may differ from the reference program's by a relative error of at most 0.025.
Values may be sent and summed in bfloat16 or wider, within the bound.
No kernel may reach another device: no remote copies, remote signals or barrier semaphores. Data moves between devices by JAX's collectives and lax.ppermute only.
A program may use at most 64 MiB of HBM per device.

```python
import math
import jax
import jax.numpy as jnp
from jax import lax

TRACE_UNKNOWNS = 128
SLOTS = 12
ROWS_PER_INDEX = 4
PARAM_DIRECTIONS = 32
OBS_DEV = 128
NBLK = 128
COLBLK = 8
NOBS = 4096
N_ROW = 32
N_COL = 16


def draw_counts(key, part):
    base = jax.random.randint(key, (NBLK, N_COL), (SLOTS + 1) // 2, SLOTS + 1)
    rows = lax.broadcasted_iota(jnp.int32, (NBLK, N_COL), 0)
    return jnp.where(rows % ROWS_PER_INDEX == 0, SLOTS, base).astype(jnp.int32)


def draw_inverse_diag(key, part):
    key_diag = jax.random.fold_in(key, 11)
    key_off = jax.random.fold_in(key, 12)
    diagonal = jax.random.uniform(key_diag, (NBLK, TRACE_UNKNOWNS), jnp.float32, 0.6, 1.4)
    offdiag = 0.45 * jax.random.normal(key_off, (NBLK, TRACE_UNKNOWNS, TRACE_UNKNOWNS), jnp.float32) / jnp.sqrt(1.0 * TRACE_UNKNOWNS)
    identity = jnp.eye(TRACE_UNKNOWNS, dtype=jnp.float32)
    return (offdiag * (1.0 - identity)[None] + diagonal[:, :, None] * identity[None]).astype(jnp.float32)


def set_ends(entries, stream_key, least, high):
    dims = entries.shape
    index_at = [jax.random.randint(jax.random.fold_in(stream_key, axis), (), 0, dims[axis]) for axis in range(len(dims))]
    entries = entries.at[tuple(index_at)].set(least)
    longest = dims.index(max(dims))
    index_at[longest] = (index_at[longest] + 1) % dims[longest]
    return entries.at[tuple(index_at)].set(high)


def levels(key, extent, shards, low, high):
    def one(axis_at, parts):
        draws = jax.random.uniform(jax.random.fold_in(jax.random.fold_in(key, 6), axis_at), (parts,), jnp.float32, low / len(shards), high / len(shards))
        return jnp.repeat(jnp.exp(draws), extent[axis_at] // parts).reshape((-1,) + (1,) * (len(extent) - axis_at - 1))

    factor_of = one(*shards[0])
    for cut in shards[1:]:
        factor_of = factor_of * one(*cut)
    return factor_of


def noise(key, extent, scale, limit, cuts=(), kind=jnp.bfloat16):
    entries = scale * jax.random.normal(key, extent, jnp.float32)
    if cuts:
        entries = entries * levels(key, extent, cuts, -0.22, 0.18)
    return jnp.clip(entries, -limit, limit).astype(kind)


def setup_inputs(seed: int = 0) -> dict:
    streams_of = jax.random.split(jax.random.key(seed), 11)
    blocks = noise(streams_of[0], (NBLK, N_COL * SLOTS, TRACE_UNKNOWNS, TRACE_UNKNOWNS), (4 * SLOTS * TRACE_UNKNOWNS) ** -0.5, 0.078125, ((0, 32), (1, 16)))
    columns = set_ends(jax.random.randint(streams_of[1], (NBLK, N_COL * SLOTS), 0, COLBLK), jax.random.fold_in(streams_of[1], 1), 0, COLBLK - 1).astype(jnp.int32)
    counts = draw_counts(jax.random.fold_in(streams_of[10], 71), 0)
    inverse_diag = draw_inverse_diag(jax.random.fold_in(streams_of[10], 71), 0)
    log_inverse_permeability = jnp.clip(jax.random.uniform(streams_of[4], (NBLK, TRACE_UNKNOWNS), jnp.float32, -1.0, 1.0) * levels(streams_of[4], (NBLK, TRACE_UNKNOWNS), ((0, 32),), -0.4, 0.0), -1.0, 1.0)
    base_velocity = noise(streams_of[5], (NBLK, TRACE_UNKNOWNS), 1.0, 6.0, ((0, 32),), jnp.float32)
    direction = noise(streams_of[6], (PARAM_DIRECTIONS, NBLK, TRACE_UNKNOWNS), 1.0, 6.0, ((1, 32),), jnp.float32)
    obs_rows = set_ends(jax.random.randint(streams_of[7], (NOBS,), 0, ROWS_PER_INDEX), jax.random.fold_in(streams_of[7], 1), 0, ROWS_PER_INDEX - 1).astype(jnp.int32)
    obs_weight = noise(streams_of[8], (NOBS, TRACE_UNKNOWNS), TRACE_UNKNOWNS ** -0.5, 0.5, ((0, 32),), jnp.float32)
    noise_prec = jnp.clip(jnp.exp(math.log(2.0) - 1.3862944 * jax.random.uniform(streams_of[9], (NOBS,), jnp.float32) ** levels(streams_of[9], (NOBS,), ((0, 32),), -0.2, 0.2)), 0.5, 2.0)
    return {"blocks": blocks, "columns": columns, "counts": counts, "inverse_diag": inverse_diag, "log_inverse_permeability": log_inverse_permeability, "base_velocity": base_velocity, "direction": direction, "obs_rows": obs_rows, "obs_weight": obs_weight, "noise_prec": noise_prec}


def diag_apply(inverse_diag, values):
    return jnp.einsum('iab,sib->sia', inverse_diag, values, precision=lax.Precision.HIGHEST)


def diag_apply_t(inverse_diag, values):
    return jnp.einsum('iba,sib->sia', inverse_diag, values, precision=lax.Precision.HIGHEST)


def reference(blocks, columns, counts, inverse_diag, log_inverse_permeability, base_velocity, direction, obs_rows, obs_weight, noise_prec):
    width = N_COL * SLOTS
    alpha_u = jnp.exp(log_inverse_permeability) * base_velocity
    forcing = -alpha_u[None] * direction
    group_of = (jnp.arange(width) // SLOTS).astype(jnp.int32)
    global_cols = (columns + group_of[None, :] * COLBLK).astype(jnp.int32)
    live = (jnp.arange(width) % SLOTS)[None, :] < jnp.repeat(counts, SLOTS, axis=1)
    block_groups = blocks.reshape(N_ROW, ROWS_PER_INDEX, width, TRACE_UNKNOWNS, TRACE_UNKNOWNS)
    col_groups = global_cols.reshape(N_ROW, ROWS_PER_INDEX, width)
    live_groups = live.reshape(N_ROW, ROWS_PER_INDEX, width)

    def apply_forward(values):
        def single_group(items):
            block_part, col_part, live_part = items
            picked = values[:, col_part].astype(jnp.float32)
            picked = jnp.where(live_part[None, :, :, None], picked, 0.0)
            return jnp.einsum('ikab,sikb->sia', block_part.astype(jnp.float32), picked)
        result = lax.map(single_group, (block_groups, col_groups, live_groups))
        return result.transpose(1, 0, 2, 3).reshape(PARAM_DIRECTIONS, NBLK, TRACE_UNKNOWNS)

    def apply_adjoint(values):
        value_groups = values.reshape(PARAM_DIRECTIONS, N_ROW, ROWS_PER_INDEX, TRACE_UNKNOWNS).transpose(1, 0, 2, 3)

        def single_group(carry, items):
            block_part, col_part, live_part, value_part = items
            terms = jnp.einsum('ikab,sia->sikb', block_part.astype(jnp.float32), value_part.astype(jnp.float32))
            terms = jnp.where(live_part[None, :, :, None], terms, 0.0)
            return carry.at[:, col_part].add(terms), None
        start = jnp.zeros((PARAM_DIRECTIONS, NBLK, TRACE_UNKNOWNS), jnp.float32)
        total, unused = lax.scan(single_group, start, (block_groups, col_groups, live_groups, value_groups))
        return total

    trace_state = diag_apply(inverse_diag, forcing)
    for sweep in range(2):
        trace_state = diag_apply(inverse_diag, forcing - apply_forward(trace_state.astype(jnp.bfloat16)))
    onehot = (obs_rows.reshape(N_ROW, OBS_DEV)[:, :, None] == jnp.arange(ROWS_PER_INDEX)[None, None, :]).astype(jnp.float32)
    weight_values = obs_weight.reshape(N_ROW, OBS_DEV, TRACE_UNKNOWNS)
    sampled_draws = jnp.einsum('zjw,fzvw->fzjv', weight_values, trace_state.reshape(PARAM_DIRECTIONS, N_ROW, ROWS_PER_INDEX, TRACE_UNKNOWNS), precision=lax.Precision.HIGHEST)
    predicted = jnp.sum(sampled_draws * onehot[None], axis=3)
    scaled = predicted * noise_prec.reshape(N_ROW, OBS_DEV)[None]
    coupling = onehot[:, :, :, None] * weight_values[:, :, None, :]
    adjoint_force = -jnp.einsum('scp,cpia->scia', scaled, coupling, precision=lax.Precision.HIGHEST).reshape(PARAM_DIRECTIONS, NBLK, TRACE_UNKNOWNS)
    adjoint = diag_apply_t(inverse_diag, adjoint_force)
    for sweep in range(2):
        adjoint = diag_apply_t(inverse_diag, adjoint_force - apply_adjoint(adjoint.astype(jnp.bfloat16)))
    hessian = -alpha_u[None] * adjoint
    return hessian, predicted.reshape(PARAM_DIRECTIONS, NOBS)
```

```python
import jax
import jax.numpy as jnp
from jax import lax
from jax.experimental import pallas as pl
from jax.experimental.pallas import tpu as pltpu
from jax.sharding import Mesh
from jax.sharding import PartitionSpec as P

AXES = ("zh", "z0", "h", "k", "l", "x")
SIZES = (4, 2, 2, 2, 4, 4)
ROW = ("zh", "z0", "h", "k")
COL = ("l", "x")
NEAR = ("z0", "h", "l", "x")
FAR = ("zh", "z0", "h", "l")
F32 = jnp.float32
BF16 = jnp.bfloat16
HIGHEST = lax.Precision.HIGHEST
VMEM = pl.BlockSpec(memory_space=pltpu.VMEM)
SMEM = pl.BlockSpec(memory_space=pltpu.SMEM)

ZH, CROSS, CORE, LCOL, XCOL = range(5)


def matmul(a, b, precision=None):
    return lax.dot_general(a, b, (((1,), (0,)), ((), ())), precision=precision, preferred_element_type=F32)


def matmul_t(a, b, precision=None):
    return lax.dot_general(a, b, (((1,), (1,)), ((), ())), precision=precision, preferred_element_type=F32)


def call(kernel, outs, scalars, arrays, scratch=(), cost=None):
    return pl.pallas_call(
        kernel,
        out_shape=[jax.ShapeDtypeStruct(shape, dtype) for shape, dtype in outs],
        in_specs=[SMEM] * len(scalars) + [VMEM] * len(arrays),
        out_specs=[VMEM] * len(outs),
        scratch_shapes=list(scratch),
        cost_estimate=cost,
    )(*scalars, *arrays)


def first_state(inverse_ref, log_ref, base_ref, direction_ref, weight_ref, onehot_ref, g_ref, low_ref, seen_ref):
    alpha_u = jnp.exp(log_ref[...]) * base_ref[...]
    seen = jnp.zeros(seen_ref.shape, F32)
    weight = weight_ref[...]
    for q in range(4):
        forcing = -alpha_u[q][None, :] * direction_ref[:, q, :]
        state = matmul_t(forcing, inverse_ref[q], HIGHEST)
        g_ref[:, q * 128 : (q + 1) * 128] = state
        low_ref[:, q * 128 : (q + 1) * 128] = state.astype(BF16)
        seen += matmul_t(state, weight, HIGHEST) * onehot_ref[q][None, :]
    seen_ref[...] = seen


def build(columns_ref, counts_ref, blocks_ref, inverse_ref, weight_ref, onehot_ref, out_ref, dense):
    for q in range(4):
        dense[...] = jnp.zeros(dense.shape, F32)

        def add(slot, carry):
            column = columns_ref[q, slot]
            dense[column] += blocks_ref[q, slot].astype(F32)
            return carry

        lax.fori_loop(0, counts_ref[q, 0], add, 0)
        for c in range(8):
            out_ref[q * 128 : (q + 1) * 128, c * 128 : (c + 1) * 128] = matmul(
                inverse_ref[q], dense[c], HIGHEST
            ).astype(BF16)
    observed = jnp.zeros((128, 1024), F32)
    for q in range(4):
        coupling = (weight_ref[...] * onehot_ref[:, q : q + 1]).astype(BF16)
        observed += matmul(coupling, out_ref[q * 128 : (q + 1) * 128, :])
        rows = 640 + 32 * q
        for part in range(4):
            out_ref[640 + part * 32 : 672 + part * 32, q * 128 : (q + 1) * 128] = coupling[part * 32 : part * 32 + 32]
    out_ref[512:640, :] = observed.astype(BF16)
    out_ref[640:768, 512:1024] = jnp.zeros((128, 512), BF16)


def put_tiles(out_ref, values, first_block, near):
    for q in range(values.shape[1] // 128):
        for half in range(2):
            tile = values[half * 8 : half * 8 + 8, q * 128 : (q + 1) * 128].astype(BF16)
            share = (first_block + q) * 2 + half
            for copy in range(4):
                out_ref[share * 4 + copy if near else copy * 16 + share] = tile


def forward_one(at_ref, first_ref, second_ref, own_ref, other_ref, g_ref, g_other_ref, out_ref, state):
    core = at_ref[CORE]
    mine, theirs = core * 4, (1 - core) * 4
    state[:, pl.ds(pl.multiple_of(core * 512, 512), 512)] = first_ref[...]
    state[:, pl.ds(pl.multiple_of((1 - core) * 512, 512), 512)] = second_ref[...]
    low = state[...]
    put_tiles(out_ref, g_ref[...] * (1.0 / 16) - matmul_t(low, own_ref[0:512, :]), mine, True)
    put_tiles(out_ref, g_other_ref[...] * (1.0 / 16) - matmul_t(low, other_ref[0:512, :]), theirs, True)


def sum_near(at_ref, in_ref, out_ref):
    first = at_ref[XCOL] * 16
    total = in_ref[first].astype(F32)
    for source in range(1, 16):
        total += in_ref[first + source].astype(F32)
    out_ref[...] = jnp.broadcast_to(total.astype(BF16)[None], out_ref.shape)


def sum_far(at_ref, in_ref, out_ref):
    first = at_ref[ZH]
    total = in_ref[first].astype(F32)
    for source in range(1, 16):
        total += in_ref[first + 4 * source].astype(F32)
    out_ref[...] = jnp.broadcast_to(total.astype(BF16)[None], out_ref.shape)


def forward_two(at_ref, in_ref, own_ref, other_ref, seen_ref, seen_other_ref, out_ref, state):
    first = at_ref[LCOL] * 16
    for block in range(8):
        for half in range(2):
            state[half * 8 : half * 8 + 8, block * 128 : (block + 1) * 128] = in_ref[first + block * 2 + half].astype(F32)
    low = state[...].astype(BF16)
    mine = seen_ref[...] * (1.0 / 16) - matmul_t(low, own_ref[512:640, :])
    theirs = seen_other_ref[...] * (1.0 / 16) - matmul_t(low, other_ref[512:640, :])
    for copy in range(16):
        out_ref[copy, :, 0:128] = mine.astype(BF16)
        out_ref[copy, :, 128:256] = theirs.astype(BF16)


def adjoint_one(at_ref, in_ref, own_ref, other_ref, noise_ref, noise_other_ref, out_ref, mine_ref, theirs_ref, force_ref):
    core = at_ref[CORE]
    predicted = in_ref[0].astype(F32)
    for source in range(1, 16):
        predicted += in_ref[source].astype(F32)
    mine_ref[...] = predicted[:, 0:128]
    theirs_ref[...] = predicted[:, 128:256]
    scaled = (predicted[:, 0:128] * noise_ref[...]).astype(BF16)
    scaled_other = (predicted[:, 128:256] * noise_other_ref[...]).astype(BF16)
    put_tiles(out_ref, matmul(scaled, own_ref[512:640, :]) + matmul(scaled_other, other_ref[512:640, :]), 0, False)
    force_ref[:, 0:512] = -matmul(scaled, own_ref[640:768, 0:512])
    force_ref[:, 512:1024] = -matmul(scaled_other, other_ref[640:768, 0:512])


def gather_rows(at_ref, in_ref, force_ref, state):
    core, cross = at_ref[CORE], at_ref[CROSS]
    for side in range(2):
        first_block = (core if side == 0 else 1 - core) * 4
        for q in range(4):
            lanes = slice(side * 512 + q * 128, side * 512 + (q + 1) * 128)
            for half in range(2):
                share = (first_block + q) * 2 + half
                state[half * 8 : half * 8 + 8, lanes] = (
                    force_ref[half * 8 : half * 8 + 8, lanes] + in_ref[share * 4 + cross].astype(F32)
                )


def adjoint_two(at_ref, in_ref, own_ref, other_ref, force_ref, out_ref, state):
    gather_rows(at_ref, in_ref, force_ref, state)
    low = state[...].astype(BF16)
    total = matmul(low[:, 0:512], own_ref[0:512, :]) + matmul(low[:, 512:1024], other_ref[0:512, :])
    put_tiles(out_ref, -total, 0, False)


def adjoint_end(at_ref, in_ref, force_ref, mine_ref, theirs_ref, state):
    gather_rows(at_ref, in_ref, force_ref, state)
    mine_ref[...] = state[:, 0:512]
    theirs_ref[...] = state[:, 512:1024]


def finish(at_ref, mine_ref, theirs_ref, inverse_ref, log_ref, base_ref, out_ref):
    alpha_u = jnp.exp(log_ref[...]) * base_ref[...]
    core = at_ref[CORE]
    for part, ref in ((core, mine_ref), (1 - core, theirs_ref)):
        for q in range(4):
            adjoint = matmul(ref[:, q * 128 : (q + 1) * 128], inverse_ref[q], HIGHEST)
            out_ref[pl.ds(part * 16, 16), q, :] = -alpha_u[q][None, :] * adjoint


def transposed(flip):
    pairs = []
    for zh in range(4):
        for cross in range(4):
            for k in range(2):
                for l in range(4):
                    for x in range(4):
                        source = (((zh * 4 + cross) * 2 + k) * 4 + l) * 4 + x
                        target = (((l * 4 + x) * 2 + (k ^ flip)) * 4 + zh) * 4 + cross
                        pairs.append((source, target))
    return pairs


def swapped(array):
    return lax.ppermute(array, "k", [(0, 1), (1, 0)])


def exchange(array, axes):
    return lax.all_to_all(array, axes, split_axis=0, concat_axis=0, tiled=True)


def per_device(
    blocks, columns, counts, inverse_diag, log_inverse_permeability, base_velocity, direction, obs_rows, obs_weight, noise_prec
):
    zh, z0, h, k, l, x = (lax.axis_index(axis) for axis in AXES)
    at = jnp.stack([zh, z0 * 2 + h, k, l, x]).astype(jnp.int32)
    onehot = (obs_rows[None, :] == jnp.arange(4)[:, None]).astype(F32)
    onehot_t = (obs_rows[:, None] == jnp.arange(4)[None, :]).astype(F32)

    g, low, seen = call(
        first_state,
        [((32, 512), F32), ((32, 512), BF16), ((32, 128), F32)],
        [],
        [inverse_diag, log_inverse_permeability, base_velocity, direction, obs_weight, onehot],
    )

    def half(array, which):
        return lax.dynamic_slice_in_dim(array, which * 16, 16, 0)

    first = lax.ppermute(half(low, k), AXES, transposed(0))
    second = lax.ppermute(half(low, 1 - k), AXES, transposed(1))
    sent = jnp.concatenate([half(g, 1 - k), half(seen, 1 - k), jnp.broadcast_to(noise_prec[None, :], (16, 128))], axis=1)
    came = swapped(sent)
    g_mine, g_other = half(g, k), came[:, 0:512]
    seen_mine, seen_other = half(seen, k), came[:, 512:640]
    noise, noise_other = noise_prec[None, :], came[0:1, 640:768]

    (own,) = call(
        build,
        [((768, 1024), BF16)],
        [columns, counts],
        [blocks, inverse_diag, obs_weight, onehot_t],
        [pltpu.VMEM((8, 128, 128), F32)],
        pl.CostEstimate(flops=2 * 10**9, bytes_accessed=4 * 10**6, transcendentals=0),
    )
    other = swapped(own)

    tiles = ((64, 8, 128), BF16)
    low_state = [pltpu.VMEM((16, 1024), BF16)]
    full_state = [pltpu.VMEM((16, 1024), F32)]
    (part,) = call(forward_one, [tiles], [at], [first, second, own, other, g_mine, g_other], low_state)
    (part,) = call(sum_near, [tiles], [at], [exchange(part, NEAR)])
    (part,) = call(
        forward_two, [((16, 16, 256), BF16)], [at], [exchange(part, FAR), own, other, seen_mine, seen_other], full_state
    )
    part, predicted, predicted_other, force = call(
        adjoint_one,
        [tiles, ((16, 128), F32), ((16, 128), F32), ((16, 1024), F32)],
        [at],
        [exchange(part, COL), own, other, noise, noise_other],
    )
    predicted_came = swapped(predicted_other)
    (part,) = call(sum_far, [tiles], [at], [exchange(part, FAR)])
    (part,) = call(adjoint_two, [tiles], [at], [exchange(part, NEAR), own, other, force], full_state)
    (part,) = call(sum_far, [tiles], [at], [exchange(part, FAR)])
    mine, theirs = call(
        adjoint_end, [((16, 512), F32), ((16, 512), F32)], [at], [exchange(part, NEAR), force], full_state
    )
    (hessian,) = call(
        finish,
        [((32, 4, 128), F32)],
        [at],
        [mine, swapped(theirs), inverse_diag, log_inverse_permeability, base_velocity],
    )
    both = jnp.where(k == 0, jnp.stack([predicted, predicted_came]), jnp.stack([predicted_came, predicted]))
    return (hessian, both.reshape(32, 128))


def solution(mesh):
    grid = Mesh(mesh.devices.reshape(SIZES), AXES)
    return jax.shard_map(
        per_device,
        mesh=grid,
        in_specs=(
            P(ROW, COL, None, None),
            P(ROW, COL),
            P(ROW, COL),
            P(ROW, None, None),
            P(ROW, None),
            P(ROW, None),
            P(None, ROW, None),
            P(ROW),
            P(ROW, None),
            P(ROW),
        ),
        out_specs=(P(None, ROW, None), P(None, ROW)),
        check_vma=False,
    )
```

```python
import jax
import jax.numpy as jnp
from jax import lax
from jax.experimental import pallas as pl
from jax.experimental.pallas import tpu as pltpu
from jax.sharding import Mesh
from jax.sharding import PartitionSpec as P

AXES = ("zh", "z0", "h", "k", "l", "x")
SIZES = (4, 2, 2, 2, 4, 4)
ROW = ("zh", "z0", "h", "k")
COL = ("l", "x")
NEAR = ("z0", "h", "l", "x")
FAR = ("zh", "z0", "h", "l")
F32 = jnp.float32
BF16 = jnp.bfloat16
HIGHEST = lax.Precision.HIGHEST
VMEM = pl.BlockSpec(memory_space=pltpu.VMEM)
SMEM = pl.BlockSpec(memory_space=pltpu.SMEM)

GRANT = 12 * 2**20


def split(array):
    high = array.astype(BF16)
    return high, (array - high.astype(F32)).astype(BF16)


def matmul(a, b, precision=None):
    return lax.dot_general(a, b, (((1,), (0,)), ((), ())), precision=precision, preferred_element_type=F32)


def matmul_t(a, b, precision=None):
    return lax.dot_general(a, b, (((1,), (1,)), ((), ())), precision=precision, preferred_element_type=F32)


def call(kernel, outs, arrays, scratch=(), scalars=(), cost=None):
    return pl.pallas_call(
        kernel,
        out_shape=[jax.ShapeDtypeStruct(shape, dtype) for shape, dtype in outs],
        in_specs=[SMEM] * len(scalars) + [VMEM] * len(arrays),
        out_specs=[VMEM] * len(outs),
        scratch_shapes=list(scratch),
        cost_estimate=cost,
        compiler_params=pltpu.CompilerParams(vmem_limit_bytes=GRANT),
    )(*scalars, *arrays)


def cross_index():
    return lax.axis_index("z0") * 2 + lax.axis_index("h")


def of_core(core, rows=16):
    return pl.ds(pl.multiple_of(core * rows, rows), rows)


def first_state(inverse_ref, log_ref, base_ref, direction_ref, g_ref, first_ref, second_ref):
    core = lax.axis_index("k")
    alpha_u = jnp.exp(log_ref[...]) * base_ref[...]
    for q in range(4):
        forcing = -alpha_u[q][None, :] * direction_ref[:, q, :]
        g_ref[:, q * 128 : (q + 1) * 128] = matmul_t(forcing, inverse_ref[q], HIGHEST)
    first_ref[...] = g_ref[of_core(core), :].astype(BF16)
    second_ref[...] = g_ref[of_core(1 - core), :].astype(BF16)


def build(columns_ref, counts_ref, blocks_ref, inverse_ref, weight_ref, rows_ref, noise_ref, g_ref, out_ref, seen_ref, dense):
    core = lax.axis_index("k")
    for q in range(4):
        dense[...] = jnp.zeros(dense.shape, F32)

        def add(slot, carry):
            lanes = pl.ds(pl.multiple_of(columns_ref[q, slot] * 128, 128), 128)
            dense[:, lanes] += blocks_ref[q, slot].astype(F32)
            return carry

        lax.fori_loop(0, counts_ref[q], add, 0)
        high, low = split(dense[...])
        inverse, inverse_low = split(inverse_ref[q])
        out_ref[q * 128 : (q + 1) * 128, :] = (
            matmul(inverse, high) + matmul(inverse, low) + matmul(inverse_low, high)
        ).astype(BF16)
    rows = rows_ref[...]
    rows_down = jnp.transpose(jnp.broadcast_to(rows.astype(F32), (128, 128)))
    weight = weight_ref[...]
    for q in range(4):
        out_ref[640:768, q * 128 : (q + 1) * 128] = jnp.where(rows_down == q, weight, 0.0).astype(BF16)
    out_ref[512:640, :] = matmul(out_ref[640:768, 0:512], out_ref[0:512, :]).astype(BF16)
    seen = jnp.zeros(seen_ref.shape, F32)
    for q in range(4):
        seen += jnp.where(rows == q, matmul_t(g_ref[:, q * 128 : (q + 1) * 128], weight, HIGHEST), 0.0)
    seen_ref[...] = seen
    out_ref[640:656, 512:1024], out_ref[656:672, 512:1024] = split(g_ref[of_core(1 - core), :])
    out_ref[672:688, 512:640], out_ref[672:688, 640:768] = split(seen_ref[of_core(1 - core), :])
    out_ref[672:688, 768:896], out_ref[672:688, 896:1024] = split(jnp.broadcast_to(noise_ref[...], (16, 128)))
    out_ref[688:768, 512:1024] = jnp.zeros((80, 512), BF16)


def joined(ref, rows, lanes, rows_low, lanes_low):
    return ref[rows, lanes].astype(F32) + ref[rows_low, lanes_low].astype(F32)


def put_tiles(out_ref, values, first_block, near):
    for q in range(values.shape[1] // 128):
        for half in range(2):
            tile = values[half * 8 : half * 8 + 8, q * 128 : (q + 1) * 128].astype(BF16)
            share = (first_block + q) * 2 + half
            for copy in range(4):
                out_ref[share * 4 + copy if near else copy * 16 + share] = tile


def forward_one(first_ref, second_ref, own_ref, other_ref, g_ref, out_ref, state):
    core = lax.axis_index("k")
    state[:, of_core(core, 512)] = first_ref[...]
    state[:, of_core(1 - core, 512)] = second_ref[...]
    low = state[...]
    g_mine = g_ref[of_core(core), :]
    g_other = joined(other_ref, slice(640, 656), slice(512, 1024), slice(656, 672), slice(512, 1024))
    put_tiles(out_ref, g_mine * (1.0 / 16) - matmul_t(low, own_ref[0:512, :]), core * 4, True)
    put_tiles(out_ref, g_other * (1.0 / 16) - matmul_t(low, other_ref[0:512, :]), (1 - core) * 4, True)


def sum_near(in_ref, out_ref):
    first = lax.axis_index("x") * 16
    total = in_ref[first].astype(F32)
    for source in range(1, 16):
        total += in_ref[first + source].astype(F32)
    out_ref[...] = jnp.broadcast_to(total.astype(BF16)[None], out_ref.shape)


def sum_far(in_ref, out_ref):
    first = lax.axis_index("zh")
    total = in_ref[first].astype(F32)
    for source in range(1, 16):
        total += in_ref[first + 4 * source].astype(F32)
    out_ref[...] = jnp.broadcast_to(total.astype(BF16)[None], out_ref.shape)


def forward_two(in_ref, own_ref, other_ref, seen_ref, out_ref, state):
    core = lax.axis_index("k")
    first = lax.axis_index("l") * 16
    for block in range(8):
        for half in range(2):
            state[half * 8 : half * 8 + 8, block * 128 : (block + 1) * 128] = in_ref[first + block * 2 + half].astype(F32)
    low = state[...].astype(BF16)
    seen_other = joined(other_ref, slice(672, 688), slice(512, 640), slice(672, 688), slice(640, 768))
    mine = seen_ref[of_core(core), :] * (1.0 / 16) - matmul_t(low, own_ref[512:640, :])
    theirs = seen_other * (1.0 / 16) - matmul_t(low, other_ref[512:640, :])
    out_ref[:, :, 0:128] = jnp.broadcast_to(mine.astype(BF16)[None], (16, 16, 128))
    out_ref[:, :, 128:256] = jnp.broadcast_to(theirs.astype(BF16)[None], (16, 16, 128))


def adjoint_one(in_ref, own_ref, other_ref, noise_ref, out_ref, predicted_ref, force_ref):
    predicted = in_ref[0].astype(F32)
    for source in range(1, 16):
        predicted += in_ref[source].astype(F32)
    predicted_ref[...] = predicted
    noise_other = joined(other_ref, slice(672, 688), slice(768, 896), slice(672, 688), slice(896, 1024))
    scaled = (predicted[:, 0:128] * noise_ref[...]).astype(BF16)
    scaled_other = (predicted[:, 128:256] * noise_other).astype(BF16)
    put_tiles(out_ref, matmul(scaled, own_ref[512:640, :]) + matmul(scaled_other, other_ref[512:640, :]), 0, False)
    force_ref[:, 0:512] = -matmul(scaled, own_ref[640:768, 0:512])
    force_ref[:, 512:1024] = -matmul(scaled_other, other_ref[640:768, 0:512])


def gather_rows(in_ref, force_ref, state):
    core, cross = lax.axis_index("k"), cross_index()
    for side in range(2):
        first_block = (core if side == 0 else 1 - core) * 4
        for q in range(4):
            lanes = slice(side * 512 + q * 128, side * 512 + (q + 1) * 128)
            for half in range(2):
                share = (first_block + q) * 2 + half
                state[half * 8 : half * 8 + 8, lanes] = (
                    force_ref[half * 8 : half * 8 + 8, lanes] + in_ref[share * 4 + cross].astype(F32)
                )


def adjoint_two(in_ref, own_ref, other_ref, force_ref, out_ref, state):
    gather_rows(in_ref, force_ref, state)
    low = state[...].astype(BF16)
    total = matmul(low[:, 0:512], own_ref[0:512, :]) + matmul(low[:, 512:1024], other_ref[0:512, :])
    put_tiles(out_ref, -total, 0, False)


def adjoint_end(in_ref, force_ref, predicted_ref, mine_ref, theirs_ref, state):
    gather_rows(in_ref, force_ref, state)
    mine_ref[...] = state[:, 0:512]
    theirs_ref[:, 0:512] = state[:, 512:1024]
    theirs_ref[:, 512:640] = predicted_ref[:, 128:256]


def finish(mine_ref, came_ref, predicted_ref, inverse_ref, log_ref, base_ref, out_ref, seen_ref):
    alpha_u = jnp.exp(log_ref[...]) * base_ref[...]
    core = lax.axis_index("k")
    seen_ref[of_core(core), :] = predicted_ref[:, 0:128]
    seen_ref[of_core(1 - core), :] = came_ref[:, 512:640]
    for part, ref in ((core, mine_ref), (1 - core, came_ref)):
        for q in range(4):
            adjoint = matmul(ref[:, q * 128 : (q + 1) * 128], inverse_ref[q], HIGHEST)
            out_ref[of_core(part), q, :] = -alpha_u[q][None, :] * adjoint


def transposed(flip):
    pairs = []
    for zh in range(4):
        for cross in range(4):
            for k in range(2):
                for l in range(4):
                    for x in range(4):
                        source = (((zh * 4 + cross) * 2 + k) * 4 + l) * 4 + x
                        target = (((l * 4 + x) * 2 + (k ^ flip)) * 4 + zh) * 4 + cross
                        pairs.append((source, target))
    return pairs


def swapped(array):
    return lax.ppermute(array, "k", [(0, 1), (1, 0)])


def exchange(array, axes):
    return lax.all_to_all(array, axes, split_axis=0, concat_axis=0, tiled=True)


def per_device(
    blocks, columns, counts, inverse_diag, log_inverse_permeability, base_velocity, direction, obs_rows, obs_weight, noise_prec
):
    rows, noise = obs_rows.reshape(1, 128), noise_prec.reshape(1, 128)
    tiles = ((64, 8, 128), BF16)
    low_state = [pltpu.VMEM((16, 1024), BF16)]
    full_state = [pltpu.VMEM((16, 1024), F32)]

    g, first, second = call(
        first_state,
        [((32, 512), F32), ((16, 512), BF16), ((16, 512), BF16)],
        [inverse_diag, log_inverse_permeability, base_velocity, direction],
    )
    first = lax.ppermute(first, AXES, transposed(0))
    second = lax.ppermute(second, AXES, transposed(1))
    own, seen = call(
        build,
        [((768, 1024), BF16), ((32, 128), F32)],
        [blocks, inverse_diag, obs_weight, rows, noise, g],
        [pltpu.VMEM((128, 1024), F32)],
        [columns, counts.reshape(4)],
        pl.CostEstimate(flops=2 * 10**9, bytes_accessed=4 * 10**6, transcendentals=0),
    )
    other = swapped(own)

    (part,) = call(forward_one, [tiles], [first, second, own, other, g], low_state)
    (part,) = call(sum_near, [tiles], [exchange(part, NEAR)])
    (part,) = call(forward_two, [((16, 16, 256), BF16)], [exchange(part, FAR), own, other, seen], full_state)
    part, predicted, force = call(
        adjoint_one,
        [tiles, ((16, 256), F32), ((16, 1024), F32)],
        [exchange(part, COL), own, other, noise],
    )
    (part,) = call(sum_far, [tiles], [exchange(part, FAR)])
    (part,) = call(adjoint_two, [tiles], [exchange(part, NEAR), own, other, force], full_state)
    (part,) = call(sum_far, [tiles], [exchange(part, FAR)])
    mine, theirs = call(
        adjoint_end, [((16, 512), F32), ((16, 640), F32)], [exchange(part, NEAR), force, predicted], full_state
    )
    return tuple(
        call(
            finish,
            [((32, 4, 128), F32), ((32, 128), F32)],
            [mine, swapped(theirs), predicted, inverse_diag, log_inverse_permeability, base_velocity],
        )
    )


def solution(mesh):
    grid = Mesh(mesh.devices.reshape(SIZES), AXES)
    return jax.shard_map(
        per_device,
        mesh=grid,
        in_specs=(
            P(ROW, COL, None, None),
            P(ROW, COL),
            P(ROW, COL),
            P(ROW, None, None),
            P(ROW, None),
            P(ROW, None),
            P(None, ROW, None),
            P(ROW),
            P(ROW, None),
            P(ROW),
        ),
        out_specs=(P(None, ROW, None), P(None, ROW)),
        check_vma=False,
    )
```

```python
import jax
import jax.numpy as jnp
from jax import lax
from jax.experimental import pallas as pl
from jax.experimental.pallas import tpu as pltpu
from jax.sharding import Mesh
from jax.sharding import PartitionSpec as P

AXES = ("zh", "z0", "h", "k", "l", "x")
SIZES = (4, 2, 2, 2, 4, 4)
ROW = ("zh", "z0", "h", "k")
COL = ("l", "x")
NEAR = ("z0", "h", "l", "x")
FAR = ("zh", "z0", "h", "l")
F32 = jnp.float32
BF16 = jnp.bfloat16
HIGHEST = lax.Precision.HIGHEST
VMEM = pl.BlockSpec(memory_space=pltpu.VMEM)
HBM = pl.BlockSpec(memory_space=pltpu.HBM)

GRANT = 12 * 2**20


def split(array):
    high = array.astype(BF16)
    return high, (array - high.astype(F32)).astype(BF16)


def matmul(a, b, precision=None):
    return lax.dot_general(a, b, (((1,), (0,)), ((), ())), precision=precision, preferred_element_type=F32)


def matmul_t(a, b, precision=None):
    return lax.dot_general(a, b, (((1,), (1,)), ((), ())), precision=precision, preferred_element_type=F32)


def call(kernel, outs, arrays, scratch=(), remote=(), cost=None):
    return pl.pallas_call(
        kernel,
        out_shape=[jax.ShapeDtypeStruct(shape, dtype) for shape, dtype in outs],
        in_specs=[HBM] * len(remote) + [VMEM] * len(arrays),
        out_specs=[VMEM] * len(outs),
        scratch_shapes=list(scratch),
        cost_estimate=cost,
        compiler_params=pltpu.CompilerParams(vmem_limit_bytes=GRANT),
    )(*(pltpu.with_memory_space_constraint(array, pltpu.HBM) for array in remote), *arrays)


def cross_index():
    return lax.axis_index("z0") * 2 + lax.axis_index("h")


def of_core(core, rows=16):
    return pl.ds(pl.multiple_of(core * rows, rows), rows)


def fetch(pairs, sems):
    copies = [pltpu.make_async_copy(source, target, sems.at[n]) for n, (source, target) in enumerate(pairs)]
    for copy in copies:
        copy.start()
    return copies


def first_state(inverse_hbm, log_hbm, base_hbm, direction_hbm, g_ref, sent_ref, inverse_ref, log_ref, base_ref, direction_ref, sems):
    copies = fetch(
        [(log_hbm, log_ref), (base_hbm, base_ref), (direction_hbm, direction_ref)]
        + [(inverse_hbm.at[q], inverse_ref.at[q]) for q in range(4)],
        sems,
    )
    core = lax.axis_index("k")
    for copy in copies[:3]:
        copy.wait()
    alpha_u = jnp.exp(log_ref[...]) * base_ref[...]
    for q in range(4):
        forcing = -alpha_u[q][None, :] * direction_ref[:, q, :]
        copies[3 + q].wait()
        g_ref[:, q * 128 : (q + 1) * 128] = matmul_t(forcing, inverse_ref[q], HIGHEST)
    sent_ref[...] = g_ref[of_core(1 - core), :]


def low_state(g_ref, came_ref, out_ref):
    core = lax.axis_index("k")
    out_ref[:, of_core(core, 512)] = g_ref[of_core(core), :].astype(BF16)
    out_ref[:, of_core(1 - core, 512)] = came_ref[...].astype(BF16)


def build(
    columns_hbm, counts_hbm, blocks_hbm, inverse_hbm, weight_hbm, rows_hbm, noise_hbm, g_ref, after_ref, out_ref, seen_ref,
    dense, columns_ref, counts_ref, blocks_ref, inverse_ref, weight_ref, rows_ref, noise_ref, sems,
):
    copies = fetch(
        [(columns_hbm, columns_ref), (counts_hbm, counts_ref), (weight_hbm, weight_ref), (rows_hbm, rows_ref), (noise_hbm, noise_ref)]
        + [(blocks_hbm.at[q], blocks_ref.at[q]) for q in range(4)]
        + [(inverse_hbm.at[q], inverse_ref.at[q]) for q in range(4)],
        sems,
    )
    core = lax.axis_index("k")
    for copy in copies[:5]:
        copy.wait()
    for q in range(4):
        dense[...] = jnp.zeros(dense.shape, F32)
        copies[5 + q].wait()

        def add(slot, carry):
            lanes = pl.ds(pl.multiple_of(columns_ref[q, slot] * 128, 128), 128)
            dense[:, lanes] += blocks_ref[q, slot].astype(F32)
            return carry

        lax.fori_loop(0, counts_ref[q], add, 0)
        high, low = split(dense[...])
        copies[9 + q].wait()
        inverse, inverse_low = split(inverse_ref[q])
        out_ref[q * 128 : (q + 1) * 128, :] = (
            matmul(inverse, high) + matmul(inverse, low) + matmul(inverse_low, high)
        ).astype(BF16)
    rows = rows_ref[...]
    rows_down = jnp.transpose(jnp.broadcast_to(rows.astype(F32), (128, 128)))
    weight = weight_ref[...]
    for q in range(4):
        out_ref[640:768, q * 128 : (q + 1) * 128] = jnp.where(rows_down == q, weight, 0.0).astype(BF16)
    out_ref[512:640, :] = matmul(out_ref[640:768, 0:512], out_ref[0:512, :]).astype(BF16)
    seen = jnp.zeros(seen_ref.shape, F32)
    for q in range(4):
        seen += jnp.where(rows == q, matmul_t(g_ref[:, q * 128 : (q + 1) * 128], weight, HIGHEST), 0.0)
    seen_ref[...] = seen
    out_ref[640:672, 512:1024] = jnp.zeros((32, 512), BF16)
    out_ref[672:688, 512:640], out_ref[672:688, 640:768] = split(seen_ref[of_core(1 - core), :])
    out_ref[672:688, 768:896], out_ref[672:688, 896:1024] = split(jnp.broadcast_to(noise_ref[...], (16, 128)))
    out_ref[688:768, 512:1024] = jnp.zeros((80, 512), BF16)


def joined(ref, rows, lanes, rows_low, lanes_low):
    return ref[rows, lanes].astype(F32) + ref[rows_low, lanes_low].astype(F32)


def put_tiles(out_ref, values, first_block, near):
    for q in range(values.shape[1] // 128):
        for half in range(2):
            tile = values[half * 8 : half * 8 + 8, q * 128 : (q + 1) * 128].astype(BF16)
            share = (first_block + q) * 2 + half
            for copy in range(4):
                out_ref[share * 4 + copy if near else copy * 16 + share] = tile


def forward_one(low_ref, own_ref, other_ref, g_ref, came_ref, out_ref):
    core = lax.axis_index("k")
    low = low_ref[...]
    g_mine = g_ref[of_core(core), :]
    put_tiles(out_ref, g_mine * (1.0 / 16) - matmul_t(low, own_ref[0:512, :]), core * 4, True)
    put_tiles(out_ref, came_ref[...] * (1.0 / 16) - matmul_t(low, other_ref[0:512, :]), (1 - core) * 4, True)


def sum_near(in_ref, out_ref):
    first = lax.axis_index("x") * 16
    total = in_ref[first].astype(F32)
    for source in range(1, 16):
        total += in_ref[first + source].astype(F32)
    out_ref[...] = jnp.broadcast_to(total.astype(BF16)[None], out_ref.shape)


def sum_far(in_ref, out_ref):
    first = lax.axis_index("zh")
    total = in_ref[first].astype(F32)
    for source in range(1, 16):
        total += in_ref[first + 4 * source].astype(F32)
    out_ref[...] = jnp.broadcast_to(total.astype(BF16)[None], out_ref.shape)


def forward_two(in_ref, own_ref, other_ref, seen_ref, out_ref, state):
    core = lax.axis_index("k")
    first = lax.axis_index("l") * 16
    for block in range(8):
        for half in range(2):
            state[half * 8 : half * 8 + 8, block * 128 : (block + 1) * 128] = in_ref[first + block * 2 + half].astype(F32)
    low = state[...].astype(BF16)
    seen_other = joined(other_ref, slice(672, 688), slice(512, 640), slice(672, 688), slice(640, 768))
    mine = seen_ref[of_core(core), :] * (1.0 / 16) - matmul_t(low, own_ref[512:640, :])
    theirs = seen_other * (1.0 / 16) - matmul_t(low, other_ref[512:640, :])
    out_ref[:, :, 0:128] = jnp.broadcast_to(mine.astype(BF16)[None], (16, 16, 128))
    out_ref[:, :, 128:256] = jnp.broadcast_to(theirs.astype(BF16)[None], (16, 16, 128))


def adjoint_one(in_ref, own_ref, other_ref, noise_ref, out_ref, predicted_ref, force_ref):
    predicted = in_ref[0].astype(F32)
    for source in range(1, 16):
        predicted += in_ref[source].astype(F32)
    predicted_ref[...] = predicted
    noise_other = joined(other_ref, slice(672, 688), slice(768, 896), slice(672, 688), slice(896, 1024))
    scaled = (predicted[:, 0:128] * noise_ref[...]).astype(BF16)
    scaled_other = (predicted[:, 128:256] * noise_other).astype(BF16)
    put_tiles(out_ref, matmul(scaled, own_ref[512:640, :]) + matmul(scaled_other, other_ref[512:640, :]), 0, False)
    force_ref[:, 0:512] = -matmul(scaled, own_ref[640:768, 0:512])
    force_ref[:, 512:1024] = -matmul(scaled_other, other_ref[640:768, 0:512])


def gather_rows(in_ref, force_ref, state):
    core, cross = lax.axis_index("k"), cross_index()
    for side in range(2):
        first_block = (core if side == 0 else 1 - core) * 4
        for q in range(4):
            lanes = slice(side * 512 + q * 128, side * 512 + (q + 1) * 128)
            for half in range(2):
                share = (first_block + q) * 2 + half
                state[half * 8 : half * 8 + 8, lanes] = (
                    force_ref[half * 8 : half * 8 + 8, lanes] + in_ref[share * 4 + cross].astype(F32)
                )


def adjoint_two(in_ref, own_ref, other_ref, force_ref, out_ref, state):
    gather_rows(in_ref, force_ref, state)
    low = state[...].astype(BF16)
    total = matmul(low[:, 0:512], own_ref[0:512, :]) + matmul(low[:, 512:1024], other_ref[0:512, :])
    put_tiles(out_ref, -total, 0, False)


def adjoint_end(in_ref, force_ref, predicted_ref, mine_ref, theirs_ref, state):
    gather_rows(in_ref, force_ref, state)
    mine_ref[...] = state[:, 0:512]
    theirs_ref[:, 0:512] = state[:, 512:1024]
    theirs_ref[:, 512:640] = predicted_ref[:, 128:256]


def finish(mine_ref, came_ref, predicted_ref, inverse_ref, log_ref, base_ref, out_ref, seen_ref):
    alpha_u = jnp.exp(log_ref[...]) * base_ref[...]
    core = lax.axis_index("k")
    seen_ref[of_core(core), :] = predicted_ref[:, 0:128]
    seen_ref[of_core(1 - core), :] = came_ref[:, 512:640]
    for part, ref in ((core, mine_ref), (1 - core, came_ref)):
        for q in range(4):
            adjoint = matmul(ref[:, q * 128 : (q + 1) * 128], inverse_ref[q], HIGHEST)
            out_ref[of_core(part), q, :] = -alpha_u[q][None, :] * adjoint


def transposed():
    pairs = []
    for zh in range(4):
        for cross in range(4):
            for k in range(2):
                for l in range(4):
                    for x in range(4):
                        source = (((zh * 4 + cross) * 2 + k) * 4 + l) * 4 + x
                        target = (((l * 4 + x) * 2 + k) * 4 + zh) * 4 + cross
                        pairs.append((source, target))
    return pairs


def swapped(array):
    return lax.ppermute(array, "k", [(0, 1), (1, 0)])


def exchange(array, axes):
    return lax.all_to_all(array, axes, split_axis=0, concat_axis=0, tiled=True)


def apply(
    blocks, columns, counts, inverse_diag, log_inverse_permeability, base_velocity, direction, obs_rows, obs_weight, noise_prec
):
    rows, noise = obs_rows.reshape(1, 128), noise_prec.reshape(1, 128)
    tiles = ((64, 8, 128), BF16)
    full_state = [pltpu.VMEM((16, 1024), F32)]

    g, sent = call(
        first_state,
        [((32, 512), F32), ((16, 512), F32)],
        [],
        [pltpu.VMEM(shape, F32) for shape in ((4, 128, 128), (4, 128), (4, 128), (32, 4, 128))] + [pltpu.SemaphoreType.DMA((7,))],
        [inverse_diag, log_inverse_permeability, base_velocity, direction],
    )
    came = swapped(sent)
    (low,) = call(low_state, [((16, 1024), BF16)], [g, came])
    turned = lax.ppermute(low, AXES, transposed())
    own, seen = call(
        build,
        [((768, 1024), BF16), ((32, 128), F32)],
        [g, low],
        [
            pltpu.VMEM((128, 1024), F32),
            pltpu.SMEM((4, 12), jnp.int32),
            pltpu.SMEM((4,), jnp.int32),
            pltpu.VMEM((4, 12, 128, 128), BF16),
            pltpu.VMEM((4, 128, 128), F32),
            pltpu.VMEM((128, 128), F32),
            pltpu.VMEM((1, 128), jnp.int32),
            pltpu.VMEM((1, 128), F32),
            pltpu.SemaphoreType.DMA((13,)),
        ],
        [columns, counts.reshape(4), blocks, inverse_diag, obs_weight, rows, noise],
        pl.CostEstimate(flops=2 * 10**9, bytes_accessed=4 * 10**6, transcendentals=0),
    )
    other = swapped(own)

    (part,) = call(forward_one, [tiles], [turned, own, other, g, came])
    (part,) = call(sum_near, [tiles], [exchange(part, NEAR)])
    (part,) = call(forward_two, [((16, 16, 256), BF16)], [exchange(part, FAR), own, other, seen], full_state)
    part, predicted, force = call(
        adjoint_one,
        [tiles, ((16, 256), F32), ((16, 1024), F32)],
        [exchange(part, COL), own, other, noise],
    )
    (part,) = call(sum_far, [tiles], [exchange(part, FAR)])
    (part,) = call(adjoint_two, [tiles], [exchange(part, NEAR), own, other, force], full_state)
    (part,) = call(sum_far, [tiles], [exchange(part, FAR)])
    mine, theirs = call(
        adjoint_end, [((16, 512), F32), ((16, 640), F32)], [exchange(part, NEAR), force, predicted], full_state
    )
    return tuple(
        call(
            finish,
            [((32, 4, 128), F32), ((32, 128), F32)],
            [mine, swapped(theirs), predicted, inverse_diag, log_inverse_permeability, base_velocity],
        )
    )


def solution(mesh):
    grid = Mesh(mesh.devices.reshape(SIZES), AXES)
    return jax.shard_map(
        apply,
        mesh=grid,
        in_specs=(
            P(ROW, COL, None, None),
            P(ROW, COL),
            P(ROW, COL),
            P(ROW, None, None),
            P(ROW, None),
            P(ROW, None),
            P(None, ROW, None),
            P(ROW),
            P(ROW, None),
            P(ROW),
        ),
        out_specs=(P(None, ROW, None), P(None, ROW)),
        check_vma=False,
    )
```
